32 devices in a mesh: dp: 4 (over y, x), mp: 8 (over z, core).
Axes of the slice: x: 2, y: 2, z: 4, core: 2. Of those that a mesh axis runs over, the one named last changes fastest.
Arguments:
- tokens: bfloat16 [1024, 4096], P('dp', 'mp'), may hold values from -6 to 6
- cotangent: bfloat16 [1024, 4096], P('dp', 'mp'), may hold values from -6 to 6
- gate_weight: bfloat16 [4096, 16384], P('dp', 'mp'), may hold values from -0.1875 to 0.1875
- up_weight: bfloat16 [4096, 16384], P('dp', 'mp'), may hold values from -0.1875 to 0.1875
- down_weight: bfloat16 [16384, 4096], P('mp', 'dp'), may hold values from -0.09375 to 0.09375
- gate_mask: int32 [32, 128], P('dp', 'mp'), may hold values from 0 to 1, as said below
- up_mask: int32 [32, 128], P('dp', 'mp'), may hold values from 0 to 1, as said below
- down_mask: int32 [128, 32], P('mp', 'dp'), may hold values from 0 to 1, as said below
Outputs:
- layer_out: bfloat16 [1024, 4096], P('dp', 'mp')
- token_grad: bfloat16 [1024, 4096], P('dp', 'mp')
- gate_grad: bfloat16 [4096, 16384], P('dp', 'mp')
- up_grad: bfloat16 [4096, 16384], P('dp', 'mp')
- down_grad: bfloat16 [16384, 4096], P('mp', 'dp')
The draws below stay inside these ranges and needn't reach their ends.
Inputs may be any that keep to these rules, and one draw needn't show every extreme that they name: `gate_mask`: each device's part of the mask (8 x 16 blocks) has 1 to 64 nonzero blocks; in every draw all parts of one index of mp, chosen by the seed, have exactly 64, the same index for the three masks. `up_mask`: each device's part of the mask (8 x 16 blocks) has 1 to 64 nonzero blocks; in every draw all parts of one index of mp, chosen by the seed, have exactly 64, the same index for the three masks. `down_mask`: each device's part of the mask (16 x 8 blocks) has 1 to 64 nonzero blocks; in every draw all parts of one index of mp, chosen by the seed, have exactly 64, the same index for the three masks.
All inputs are finite; a program needn't handle non-finite values.
Results may differ from the reference program's by a relative error of at most 0.017.
Values may be sent and summed in bfloat16 or wider, within the bound.
No kernel may reach another device: no remote copies, remote signals or barrier semaphores. Data moves between devices by JAX's collectives and lax.ppermute only.
A program may use at most 192 MiB of HBM per device.

```python
import math
import jax
import jax.numpy as jnp
from jax import lax

D = 4096
F = 16384
BLK = 128
TOK_DEV = 256
TOKENS = 1024
ROW_TILES = 8
COL_TILES = 16
CAP = 64


def live_tiles(key, salt_value):
    dp_shards = D // BLK // ROW_TILES
    mp_shards = F // BLK // COL_TILES
    tile_total = ROW_TILES * COL_TILES
    own_key = jax.random.fold_in(key, salt_value)
    counts = jax.random.randint(jax.random.fold_in(own_key, 1), (dp_shards, mp_shards), 1, CAP)
    full_column = jax.random.randint(jax.random.fold_in(key, 101), (), 0, mp_shards)
    counts = jnp.where(jnp.arange(mp_shards)[None, :] == full_column, CAP, counts)
    scores = jax.random.randint(jax.random.fold_in(own_key, 2), (dp_shards, mp_shards, tile_total), 0, 1048576)
    scores = scores * tile_total + jnp.arange(tile_total, dtype=jnp.int32)[None, None, :]
    ranking = jnp.argsort(jnp.argsort(scores, axis=-1), axis=-1)
    return (ranking < counts[:, :, None]).astype(jnp.int32)


def upper_layout(key, salt_value):
    dp_shards = D // BLK // ROW_TILES
    mp_shards = F // BLK // COL_TILES
    grid = live_tiles(key, salt_value).reshape(dp_shards, mp_shards, ROW_TILES, COL_TILES)
    return grid.transpose(0, 2, 1, 3).reshape(D // BLK, F // BLK)


def draw_gate_mask(key, part):
    return upper_layout(key, 1)


def draw_up_mask(key, part):
    return upper_layout(key, 2)


def draw_down_mask(key, part):
    dp_shards = D // BLK // ROW_TILES
    mp_shards = F // BLK // COL_TILES
    grid = live_tiles(key, 3).reshape(dp_shards, mp_shards, COL_TILES, ROW_TILES)
    return grid.transpose(1, 2, 0, 3).reshape(F // BLK, D // BLK)


def steps_of(rng, dims, pieces, low, largest):
    factor_of, own = 1.0, jax.random.fold_in(rng, 6)
    for axis_at, blocks in pieces:
        heights = jnp.exp(jax.random.uniform(jax.random.fold_in(own, axis_at), (blocks,), jnp.float32, low / len(pieces), largest / len(pieces)))
        factor_of = factor_of * jnp.repeat(heights, dims[axis_at] // blocks).reshape([-1 if axis == axis_at else 1 for axis in range(len(dims))])
    return factor_of


def noise(key, extent, spread, most, split=(), kind=jnp.bfloat16):
    array = spread * jax.random.normal(key, extent, jnp.float32)
    if split:
        array = array * steps_of(key, extent, split, -0.22, 0.18)
    return jnp.clip(array, -most, most).astype(kind)


def setup_inputs(seed: int = 0) -> dict:
    streams_of = jax.random.split(jax.random.key(seed), 9)
    tokens = noise(streams_of[0], (TOKENS, D), 1.0, 6.0, ((0, 4), (1, 8)))
    cotangent = noise(streams_of[1], (TOKENS, D), 1.0, 6.0, ((0, 4), (1, 8)))
    gate_weight = noise(streams_of[2], (D, F), (D // 4) ** -0.5, 0.1875, ((0, 4), (1, 8)))
    up_weight = noise(streams_of[3], (D, F), (D // 4) ** -0.5, 0.1875, ((0, 4), (1, 8)))
    down_weight = noise(streams_of[4], (F, D), (F // 4) ** -0.5, 0.09375, ((0, 8), (1, 4)))
    gate_mask = draw_gate_mask(jax.random.fold_in(streams_of[8], 71), 0)
    up_mask = draw_up_mask(jax.random.fold_in(streams_of[8], 71), 0)
    down_mask = draw_down_mask(jax.random.fold_in(streams_of[8], 71), 0)
    return dict(tokens=tokens, cotangent=cotangent, gate_weight=gate_weight, up_weight=up_weight, down_weight=down_weight, gate_mask=gate_mask, up_mask=up_mask, down_mask=down_mask)


def expand(mask_table):
    return jnp.repeat(jnp.repeat(mask_table, BLK, axis=0), BLK, axis=1).astype(jnp.bfloat16)

def rounded(values):
    lowered = values.astype(jnp.bfloat16)
    lowered = lax.optimization_barrier(lowered)
    return lowered.astype(jnp.float32)

def reference(tokens, cotangent, gate_weight, up_weight, down_weight, gate_mask, up_mask, down_mask):
    gate_eff = gate_weight * expand(gate_mask)
    up_eff = up_weight * expand(up_mask)
    down_eff = down_weight * expand(down_mask)
    gate_pre = jnp.dot(tokens, gate_eff, preferred_element_type=jnp.float32)
    up_pre = jnp.dot(tokens, up_eff, preferred_element_type=jnp.float32)
    sigmoid_gate = 1.0 / (1.0 + jnp.exp(-gate_pre))
    activated = gate_pre * sigmoid_gate
    hidden = (activated * up_pre).astype(jnp.bfloat16)
    layer_out = jnp.dot(hidden, down_eff, preferred_element_type=jnp.float32).astype(jnp.bfloat16)
    hidden_grad = jnp.dot(cotangent, down_eff.T, preferred_element_type=jnp.float32)
    gate_delta = (hidden_grad * up_pre * sigmoid_gate * (1.0 + gate_pre * (1.0 - sigmoid_gate))).astype(jnp.bfloat16)
    up_delta = (hidden_grad * activated).astype(jnp.bfloat16)
    token_grad = (jnp.dot(gate_delta, gate_eff.T, preferred_element_type=jnp.float32) + jnp.dot(up_delta, up_eff.T, preferred_element_type=jnp.float32)).astype(jnp.bfloat16)

    def group_terms(totals, group_index):
        first_row = (group_index * TOK_DEV).astype(jnp.int32)
        rows_in = lax.dynamic_slice_in_dim(tokens, first_row, TOK_DEV, 0)
        rows_cot = lax.dynamic_slice_in_dim(cotangent, first_row, TOK_DEV, 0)
        rows_gate = lax.dynamic_slice_in_dim(gate_delta, first_row, TOK_DEV, 0)
        rows_up = lax.dynamic_slice_in_dim(up_delta, first_row, TOK_DEV, 0)
        rows_hidden = lax.dynamic_slice_in_dim(hidden, first_row, TOK_DEV, 0)
        part_gate = rounded(jnp.dot(rows_in.T, rows_gate, preferred_element_type=jnp.float32))
        part_up = rounded(jnp.dot(rows_in.T, rows_up, preferred_element_type=jnp.float32))
        part_down = rounded(jnp.dot(rows_hidden.T, rows_cot, preferred_element_type=jnp.float32))
        return ((totals[0] + part_gate, totals[1] + part_up, totals[2] + part_down), None)
    initial = (jnp.zeros((D, F), jnp.float32), jnp.zeros((D, F), jnp.float32), jnp.zeros((F, D), jnp.float32))
    group_count = TOKENS // TOK_DEV
    totals, _ = lax.scan(group_terms, initial, jnp.arange(group_count, dtype=jnp.int32))
    grad_scale = 1.0 / math.sqrt(TOKENS)
    gate_grad = (totals[0] * grad_scale * expand(gate_mask).astype(jnp.float32)).astype(jnp.bfloat16)
    up_grad = (totals[1] * grad_scale * expand(up_mask).astype(jnp.float32)).astype(jnp.bfloat16)
    down_grad = (totals[2] * grad_scale * expand(down_mask).astype(jnp.float32)).astype(jnp.bfloat16)
    return (layer_out, token_grad, gate_grad, up_grad, down_grad)
```

```python
import math

import jax
import jax.numpy as jnp
from jax import lax
from jax.sharding import PartitionSpec as P

BLK = 128
DP_MODE = "permute"


def spread(mask, width):
    rows, cols = mask.shape
    lane_block = lax.broadcasted_iota(jnp.int32, (cols, width), 1) // (width // cols)
    pick = (lane_block == lax.broadcasted_iota(jnp.int32, (cols, width), 0)).astype(jnp.bfloat16)
    wide = jnp.dot(mask.astype(jnp.bfloat16), pick, preferred_element_type=jnp.float32)
    wide = wide.astype(jnp.bfloat16)
    return jnp.broadcast_to(wide[:, None, :], (rows, BLK, width)).reshape(rows * BLK, width)


def partner(value, bit, dp):
    return lax.ppermute(value, "dp", [(i, i ^ (1 << bit)) for i in range(dp)])


def reduce_over_dp(part, dp, colors=2):
    bits = dp.bit_length() - 1
    cols = part.shape[2] // colors
    done = []
    for color in range(colors):
        order = list(range(bits))
        if color % 2:
            order = order[::-1]
        piece = part[:, :, color * cols : (color + 1) * cols]
        held = list(range(dp))
        vals = {k: piece[k] for k in held}
        for bit in order:
            send = [k for k in held if k >> bit & 1]
            keep = [k for k in held if not k >> bit & 1]
            got = partner(jnp.stack([vals[k].astype(jnp.bfloat16) for k in send]), bit, dp)
            vals = {
                k ^ (1 << bit): vals[k ^ (1 << bit)].astype(jnp.float32) + got[n].astype(jnp.float32)
                for n, k in enumerate(send)
            }
            held = keep
        done.append(vals[0])
    return jnp.concatenate(done, axis=1)


def gather_over_dp(own, dp, colors=2):
    bits = dp.bit_length() - 1
    cols = own.shape[1] // colors
    done = []
    for color in range(colors):
        order = list(range(bits))[::-1]
        if color % 2:
            order = order[::-1]
        vals = {0: own[:, color * cols : (color + 1) * cols]}
        for bit in order:
            held = sorted(vals)
            got = partner(jnp.stack([vals[k] for k in held]), bit, dp)
            for n, k in enumerate(held):
                vals[k ^ (1 << bit)] = got[n]
        done.append(jnp.concatenate([vals[k] for k in range(dp)], axis=0))
    return jnp.concatenate(done, axis=1)


def body(tokens, cotangent, gate_weight, up_weight, down_weight, gate_mask, up_mask, down_mask):
    dp = lax.axis_size("dp")
    mp = lax.axis_size("mp")
    ratio = mp // dp
    rows, cols = tokens.shape
    fan = gate_weight.shape[1]
    bf16, f32 = jnp.bfloat16, jnp.float32
    there = []
    for i in range(dp):
        for j in range(mp):
            d, c = j // ratio, j % ratio
            there.append((i * mp + j, d * mp + ratio * (i ^ d) + c))
    back = [(b, a) for a, b in there]

    def spread_rows(block):
        moved = lax.ppermute(block, ("dp", "mp"), there)
        full = lax.all_gather(moved, "mp", axis=0, tiled=False)
        full = full.reshape(dp, ratio, rows, cols).transpose(0, 2, 1, 3)
        return full.reshape(dp * rows, ratio * cols)

    def collect_rows(part):
        part = part.astype(bf16).reshape(dp, rows, ratio, cols).transpose(0, 2, 1, 3)
        own = lax.psum_scatter(
            part.reshape(mp * rows, cols), "mp", scatter_dimension=0, tiled=True
        )
        return lax.ppermute(own, ("dp", "mp"), back)

    def reduce_dp(part):
        part = part.astype(bf16)
        if DP_MODE == "permute":
            return reduce_over_dp(part.reshape(dp, rows, fan), dp)
        me = lax.axis_index("dp")
        part = part.reshape(dp, rows, fan)[jnp.arange(dp) ^ me]
        return lax.psum_scatter(
            part.reshape(dp * rows, fan), "dp", scatter_dimension=0, tiled=True
        ).astype(f32)

    def gather_dp(own):
        if DP_MODE == "permute":
            return gather_over_dp(own, dp)
        me = lax.axis_index("dp")
        full = lax.all_gather(own, "dp", axis=0, tiled=False)
        return full[jnp.arange(dp) ^ me].reshape(dp * rows, fan)

    gate_keep = spread(gate_mask, fan)
    up_keep = spread(up_mask, fan)
    down_keep = spread(down_mask, down_weight.shape[1])
    gate_eff = gate_weight * gate_keep
    up_eff = up_weight * up_keep
    down_eff = down_weight * down_keep

    tok = spread_rows(tokens)
    cot = spread_rows(cotangent)
    last = (((1,), (1,)), ((), ()))
    first = (((0,), (0,)), ((), ()))

    def dot(a, b, dims=(((1,), (0,)), ((), ()))):
        return lax.dot_general(a, b, dims, preferred_element_type=f32)

    gate_pre = reduce_dp(dot(tok, gate_eff))
    up_pre = reduce_dp(dot(tok, up_eff))
    hidden_grad = reduce_dp(dot(cot, down_eff, last))
    sigmoid_gate = 1.0 / (1.0 + jnp.exp(-gate_pre))
    activated = gate_pre * sigmoid_gate
    hidden = gather_dp((activated * up_pre).astype(bf16))
    gate_delta = gather_dp(
        (hidden_grad * up_pre * sigmoid_gate * (1.0 + gate_pre * (1.0 - sigmoid_gate))).astype(bf16)
    )
    up_delta = gather_dp((hidden_grad * activated).astype(bf16))
    layer_out = collect_rows(dot(hidden, down_eff))
    token_grad = collect_rows(dot(gate_delta, gate_eff, last) + dot(up_delta, up_eff, last))
    scale = 1.0 / math.sqrt(rows * dp)
    gate_grad = (dot(tok, gate_delta, first) * scale * gate_keep.astype(f32)).astype(bf16)
    up_grad = (dot(tok, up_delta, first) * scale * up_keep.astype(f32)).astype(bf16)
    down_grad = (dot(hidden, cot, first) * scale * down_keep.astype(f32)).astype(bf16)
    return (layer_out, token_grad, gate_grad, up_grad, down_grad)


def solution(mesh):
    placed = (
        P("dp", "mp"),
        P("dp", "mp"),
        P("dp", "mp"),
        P("dp", "mp"),
        P("mp", "dp"),
        P("dp", "mp"),
        P("dp", "mp"),
        P("mp", "dp"),
    )
    return jax.shard_map(
        body,
        mesh=mesh,
        in_specs=placed,
        out_specs=(P("dp", "mp"), P("dp", "mp"), P("dp", "mp"), P("dp", "mp"), P("mp", "dp")),
        check_vma=False,
    )
```

```python
import functools
import math

import jax
import jax.numpy as jnp
from jax import lax
from jax.experimental import pallas as pl
from jax.experimental.pallas import tpu as pltpu
from jax.sharding import PartitionSpec as P

BLK = 128
COLORS = 2
bf16, f32 = jnp.bfloat16, jnp.float32
NN = (((1,), (0,)), ((), ()))
NT = (((1,), (1,)), ((), ()))
TN = (((0,), (0,)), ((), ()))


def dot(a, b, dims):
    return lax.dot_general(a, b, dims, preferred_element_type=f32)


def keep_blocks(dst, value_of, mask, row0, col0):
    for rb in range(dst.shape[0] // BLK):
        for cb in range(dst.shape[1] // BLK):
            at = (slice(rb * BLK, (rb + 1) * BLK), slice(cb * BLK, (cb + 1) * BLK))
            block = value_of(at)
            dst[at] = jnp.where(mask[row0 + rb, col0 + cb] != 0, block, jnp.zeros_like(block))


def load_groups(parts, held, sems, rows, half):
    copies = []
    groups = len(parts) // COLORS
    for n, part in enumerate(parts):
        color, k = divmod(n, groups)
        dst = held.at[pl.ds(k * rows, rows), pl.ds(color * half, half)]
        copies.append(pltpu.make_async_copy(part, dst, sems.at[n]))
    for copy in copies:
        copy.start()
    for copy in copies:
        copy.wait()


def call(kernel, grid, prefetch, in_specs, out_specs, out_shape, scratch, flops, nbytes, args):
    return pl.pallas_call(
        kernel,
        grid_spec=pltpu.PrefetchScalarGridSpec(
            num_scalar_prefetch=len(prefetch),
            grid=grid,
            in_specs=in_specs,
            out_specs=out_specs,
            scratch_shapes=scratch,
        ),
        out_shape=out_shape,
        compiler_params=pltpu.CompilerParams(
            dimension_semantics=("arbitrary",) * len(grid), vmem_limit_bytes=48 << 20
        ),
        cost_estimate=pl.CostEstimate(flops=flops, transcendentals=0, bytes_accessed=nbytes),
    )(*prefetch, *args)


def whole_spec(shape):
    return pl.BlockSpec(shape, lambda *_: (0,) * len(shape))


ANY = pl.BlockSpec(memory_space=pl.ANY)


def project(x, weight, mask, color, turned):
    groups, r, rows, cols = x.shape
    depth, fan = weight.shape[::-1] if turned else weight.shape
    half = fan // COLORS
    tile = min(half, 512)
    base = color * half // tile

    def kernel(mask_ref, x_ref, w_ref, *rest):
        outs, kept = rest[:groups], rest[groups]
        first = (base + pl.program_id(0)) * (tile // BLK)
        if turned:
            keep_blocks(kept, lambda at: w_ref[at], mask_ref, first, 0)
        else:
            keep_blocks(kept, lambda at: w_ref[at], mask_ref, 0, first)
        total = None
        for c in range(r):
            left = x_ref[:, c].reshape(groups * rows, cols)
            span = slice(c * cols, (c + 1) * cols)
            term = dot(left, kept[:, span], NT) if turned else dot(left, kept[span, :], NN)
            total = term if total is None else total + term
        for k in range(groups):
            outs[k][...] = total[k * rows : (k + 1) * rows].astype(bf16)

    shape = (tile, depth) if turned else (depth, tile)
    index = (lambda n, m: (base + n, 0)) if turned else (lambda n, m: (0, base + n))
    return call(
        kernel,
        (half // tile,),
        [mask],
        [whole_spec(x.shape), pl.BlockSpec(shape, index)],
        [pl.BlockSpec((rows, tile), lambda n, m: (0, n))] * groups,
        [jax.ShapeDtypeStruct((rows, half), bf16)] * groups,
        [pltpu.VMEM(shape, bf16)],
        2 * groups * rows * depth * half,
        2 * (groups * rows * depth + depth * half + groups * rows * half),
        [x, weight],
    )


def back_project(sets, weights, masks, place, r, turned):
    groups = len(sets[0]) // COLORS
    rows, half = sets[0][0].shape
    fan = half * COLORS
    depth = weights[0].shape[0] if turned else weights[0].shape[1]
    cols = depth // r
    tile = min(cols, 256)
    sub = cols // tile
    count = len(weights)
    parts = len(sets[0])

    def tile_at(s, u, place_ref):
        return (s ^ place_ref[0]) * sub + u

    def kernel(place_ref, *rest):
        mask_refs, rest = rest[:count], rest[count:]
        part_refs, rest = rest[: count * parts], rest[count * parts :]
        w_refs, rest = rest[:count], rest[count:]
        out, rest = rest[0], rest[1:]
        helds, kepts, sems = rest[:count], rest[count : 2 * count], rest[2 * count]
        s, u = pl.program_id(0), pl.program_id(1)

        @pl.when((s == 0) & (u == 0))
        def _():
            for i in range(count):
                load_groups(
                    part_refs[i * parts : (i + 1) * parts], helds[i], sems.at[i], rows, half
                )

        first = tile_at(s, u, place_ref) * (tile // BLK)
        total = None
        for i in range(count):
            w_ref = w_refs[i]
            if turned:
                keep_blocks(kepts[i], lambda at: w_ref[at], mask_refs[i], first, 0)
            else:
                keep_blocks(kepts[i], lambda at: w_ref[at], mask_refs[i], 0, first)
            term = dot(helds[i][...], kepts[i][...], NT if turned else NN)
            total = term if total is None else total + term
        out[0] = total.astype(bf16).reshape(groups, rows, tile)

    shape = (tile, fan) if turned else (fan, tile)
    if turned:
        index = lambda s, u, pr, *_: (tile_at(s, u, pr), 0)
    else:
        index = lambda s, u, pr, *_: (0, tile_at(s, u, pr))
    return call(
        kernel,
        (r, sub),
        [place] + masks,
        [ANY] * (count * parts) + [pl.BlockSpec(shape, index)] * count,
        pl.BlockSpec((1, groups, rows, tile), lambda s, u, *_: (s, 0, 0, u)),
        jax.ShapeDtypeStruct((r, groups, rows, cols), bf16),
        [pltpu.VMEM((groups * rows, fan), bf16)] * count
        + [pltpu.VMEM(shape, bf16)] * count
        + [pltpu.SemaphoreType.DMA((count, parts))],
        2 * count * groups * rows * depth * fan,
        2 * count * (groups * rows * fan + depth * fan) + 2 * groups * rows * depth,
        [p for group in sets for p in group] + list(weights),
    )


def outer_up(x, parts, mask, scale):
    groups, r, rows, cols = x.shape
    half = parts[0].shape[1]
    fan, depth = half * COLORS, r * cols
    tile = min(cols, 256)
    sub = cols // tile

    def kernel(mask_ref, x_ref, *rest):
        part_refs, (out, held, sems) = rest[: len(parts)], rest[len(parts) :]
        n = pl.program_id(0)

        @pl.when(n == 0)
        def _():
            load_groups(part_refs, held, sems, rows, half)

        left = x_ref[:, 0].reshape(groups * rows, tile)
        value = dot(left, held[...], TN) * scale
        keep_blocks(out, lambda at: value[at].astype(bf16), mask_ref, n * (tile // BLK), 0)

    return call(
        kernel,
        (depth // tile,),
        [mask],
        [pl.BlockSpec((groups, 1, rows, tile), lambda n, m: (0, n // sub, 0, n % sub))]
        + [ANY] * len(parts),
        pl.BlockSpec((tile, fan), lambda n, m: (n, 0)),
        jax.ShapeDtypeStruct((depth, fan), bf16),
        [pltpu.VMEM((groups * rows, fan), bf16), pltpu.SemaphoreType.DMA((len(parts),))],
        2 * groups * rows * depth * fan,
        2 * (groups * rows * (depth + fan) + depth * fan),
        [x] + list(parts),
    )


def outer_down(parts, x, mask, scale):
    groups, r, rows, cols = x.shape
    half = parts[0].shape[1]
    fan, depth = half * COLORS, r * cols
    tile = min(fan, 256)

    def kernel(mask_ref, x_ref, *rest):
        part_refs, (out, held, sems) = rest[: len(parts)], rest[len(parts) :]
        n = pl.program_id(0)

        @pl.when(n == 0)
        def _():
            load_groups(part_refs, held, sems, rows, half)

        left = held[:, pl.ds(pl.multiple_of(n * tile, tile), tile)]
        for c in range(r):
            value = dot(left, x_ref[:, c].reshape(groups * rows, cols), TN) * scale
            keep_blocks(
                out.at[:, pl.ds(c * cols, cols)],
                lambda at: value[at].astype(bf16),
                mask_ref,
                n * (tile // BLK),
                c * (cols // BLK),
            )

    return call(
        kernel,
        (fan // tile,),
        [mask],
        [whole_spec(x.shape)] + [ANY] * len(parts),
        pl.BlockSpec((tile, depth), lambda n, m: (n, 0)),
        jax.ShapeDtypeStruct((fan, depth), bf16),
        [pltpu.VMEM((groups * rows, fan), bf16), pltpu.SemaphoreType.DMA((len(parts),))],
        2 * groups * rows * depth * fan,
        2 * (groups * rows * (depth + fan) + depth * fan),
        [x] + list(parts),
    )


def assemble(pieces, where, groups, r):
    rows, cols = pieces[0][0].shape
    flat = [p for line in pieces for p in line]

    def kernel(where_ref, *rest):
        refs, (out, sems) = rest[: len(flat)], rest[len(flat) :]
        copies = []
        for n, ref in enumerate(refs):
            s, t = divmod(n, groups)
            dst = out.at[where_ref[0] ^ t, where_ref[1] ^ s]
            copies.append(pltpu.make_async_copy(ref, dst, sems.at[n]))
        for copy in copies:
            copy.start()
        for copy in copies:
            copy.wait()

    return call(
        kernel,
        (1,),
        [where],
        [ANY] * len(flat),
        ANY,
        jax.ShapeDtypeStruct((groups, r, rows, cols), bf16),
        [pltpu.SemaphoreType.DMA((len(flat),))],
        0,
        4 * len(flat) * rows * cols,
        flat,
    )


def body(tokens, cotangent, gate_weight, up_weight, down_weight, gate_mask, up_mask, down_mask):
    dp = lax.axis_size("dp")
    mp = lax.axis_size("mp")
    ratio = mp // dp
    bits = dp.bit_length() - 1
    rows = tokens.shape[0]
    scale = 1.0 / math.sqrt(rows * dp)
    there = []
    for i in range(dp):
        for j in range(mp):
            d, c = j // ratio, j % ratio
            there.append((i * mp + j, d * mp + ratio * (i ^ d) + c))
    back = [(b, a) for a, b in there]
    me = lax.axis_index("mp")
    my_k, my_c = me // ratio, me % ratio
    where = jnp.stack([my_k, my_c]).astype(jnp.int32)
    place = my_c.reshape(1).astype(jnp.int32)

    def over_mp(value, step):
        return lax.ppermute(value, "mp", [(j, j ^ step) for j in range(mp)])

    def over_dp(value, bit):
        return lax.ppermute(value, "dp", [(i, i ^ (1 << bit)) for i in range(dp)])

    def spread_rows(block):
        moved = lax.ppermute(block, ("dp", "mp"), there)
        line = [moved] + [over_mp(moved, ratio * t) for t in range(1, dp)]
        pieces = [line] + [[over_mp(v, s) for v in line] for s in range(1, ratio)]
        return assemble(pieces, where, dp, ratio)

    def collect_rows(part):
        total = part[0].astype(f32)
        for s in range(1, ratio):
            total = total + over_mp(part[s], s).astype(f32)
        total = total.astype(bf16)
        own = lax.dynamic_index_in_dim(total, my_k, 0, keepdims=False).astype(f32)
        for t in range(1, dp):
            sent = lax.dynamic_index_in_dim(total, my_k ^ t, 0, keepdims=False)
            own = own + over_mp(sent, ratio * t).astype(f32)
        return lax.ppermute(own.astype(bf16), ("dp", "mp"), back)

    def reduce_dp(parts, color):
        order = list(range(bits)) if color % 2 == 0 else list(range(bits))[::-1]
        vals = {k: parts[k] for k in range(dp)}
        for bit in order:
            for k in sorted((k for k in vals if k >> bit & 1), reverse=True):
                got = over_dp(vals.pop(k).astype(bf16), bit)
                vals[k ^ (1 << bit)] = vals[k ^ (1 << bit)].astype(f32) + got.astype(f32)
        return vals[0]

    def gather_dp(own, color):
        order = list(range(bits))[::-1] if color % 2 == 0 else list(range(bits))
        vals = {0: own}
        for bit in order:
            for k in sorted(vals):
                vals[k ^ (1 << bit)] = over_dp(vals[k], bit)
        return [vals[k] for k in range(dp)]

    tok = spread_rows(tokens)
    cot = spread_rows(cotangent)
    colors = range(COLORS)
    gate_pre = [reduce_dp(project(tok, gate_weight, gate_mask, h, False), h) for h in colors]
    up_pre = [reduce_dp(project(tok, up_weight, up_mask, h, False), h) for h in colors]
    hidden_grad = [reduce_dp(project(cot, down_weight, down_mask, h, True), h) for h in colors]
    hidden, gate_delta, up_delta = [], [], []
    for h in colors:
        gate = gate_pre[h]
        sigmoid_gate = 1.0 / (1.0 + jnp.exp(-gate))
        activated = gate * sigmoid_gate
        hidden += gather_dp((activated * up_pre[h]).astype(bf16), h)
        slope = sigmoid_gate * (1.0 + gate * (1.0 - sigmoid_gate))
        gate_delta += gather_dp((hidden_grad[h] * up_pre[h] * slope).astype(bf16), h)
        up_delta += gather_dp((hidden_grad[h] * activated).astype(bf16), h)
    layer_out = collect_rows(
        back_project([hidden], [down_weight], [down_mask], place, ratio, False)
    )
    token_grad = collect_rows(
        back_project(
            [gate_delta, up_delta],
            [gate_weight, up_weight],
            [gate_mask, up_mask],
            place,
            ratio,
            True,
        )
    )
    gate_grad = outer_up(tok, gate_delta, gate_mask, scale)
    up_grad = outer_up(tok, up_delta, up_mask, scale)
    down_grad = outer_down(hidden, cot, down_mask, scale)
    return (layer_out, token_grad, gate_grad, up_grad, down_grad)


def solution(mesh):
    placed = (
        P("dp", "mp"),
        P("dp", "mp"),
        P("dp", "mp"),
        P("dp", "mp"),
        P("mp", "dp"),
        P("dp", "mp"),
        P("dp", "mp"),
        P("mp", "dp"),
    )
    return jax.shard_map(
        body,
        mesh=mesh,
        in_specs=placed,
        out_specs=(P("dp", "mp"), P("dp", "mp"), P("dp", "mp"), P("dp", "mp"), P("mp", "dp")),
        check_vma=False,
    )
```

```python
import functools
import math

import jax
import jax.numpy as jnp
from jax import lax
from jax.experimental import pallas as pl
from jax.experimental.pallas import tpu as pltpu
from jax.sharding import PartitionSpec as P

BLK = 128
COLORS = 2
bf16, f32 = jnp.bfloat16, jnp.float32
NN = (((1,), (0,)), ((), ()))
NT = (((1,), (1,)), ((), ()))
TN = (((0,), (0,)), ((), ()))


DEPTH = 2


def after(value, *earlier):
    return lax.optimization_barrier((value,) + earlier)[0]


def dot(a, b, dims):
    return lax.dot_general(a, b, dims, preferred_element_type=f32)


def keep_blocks(dst, value_of, mask, row0, col0):
    for rb in range(dst.shape[0] // BLK):
        for cb in range(dst.shape[1] // BLK):
            at = (slice(rb * BLK, (rb + 1) * BLK), slice(cb * BLK, (cb + 1) * BLK))
            block = value_of(at)
            dst[at] = jnp.where(mask[row0 + rb, col0 + cb] != 0, block, jnp.zeros_like(block))


def load_groups(parts, held, sems, rows, half):
    copies = []
    groups = len(parts) // COLORS
    for n, part in enumerate(parts):
        color, k = divmod(n, groups)
        dst = held.at[pl.ds(k * rows, rows), pl.ds(color * half, half)]
        copies.append(pltpu.make_async_copy(part, dst, sems.at[n]))
    for copy in copies:
        copy.start()
    for copy in copies:
        copy.wait()


def call(kernel, grid, prefetch, in_specs, out_specs, out_shape, scratch, flops, nbytes, args, limit=40000):
    return pl.pallas_call(
        kernel,
        grid_spec=pltpu.PrefetchScalarGridSpec(
            num_scalar_prefetch=len(prefetch),
            grid=grid,
            in_specs=in_specs,
            out_specs=out_specs,
            scratch_shapes=scratch,
        ),
        out_shape=out_shape,
        compiler_params=pltpu.CompilerParams(
            dimension_semantics=("arbitrary",) * len(grid), vmem_limit_bytes=limit << 10
        ),
        cost_estimate=pl.CostEstimate(flops=flops, transcendentals=0, bytes_accessed=nbytes),
    )(*prefetch, *args)


def whole_spec(shape):
    return pl.BlockSpec(shape, lambda *_: (0,) * len(shape))


ANY = pl.BlockSpec(memory_space=pl.ANY)


def project(x, weight, mask, color, turned):
    groups, r, rows, cols = x.shape
    depth, fan = weight.shape[::-1] if turned else weight.shape
    half = fan // COLORS
    tile = min(half, 512)
    base = color * half // tile

    def kernel(mask_ref, x_ref, w_ref, *rest):
        outs, kept = rest[:groups], rest[groups]
        first = (base + pl.program_id(0)) * (tile // BLK)
        if turned:
            keep_blocks(kept, lambda at: w_ref[at], mask_ref, first, 0)
        else:
            keep_blocks(kept, lambda at: w_ref[at], mask_ref, 0, first)
        total = None
        for c in range(r):
            left = x_ref[:, c].reshape(groups * rows, cols)
            span = slice(c * cols, (c + 1) * cols)
            term = dot(left, kept[:, span], NT) if turned else dot(left, kept[span, :], NN)
            total = term if total is None else total + term
        for k in range(groups):
            outs[k][...] = total[k * rows : (k + 1) * rows].astype(bf16)

    shape = (tile, depth) if turned else (depth, tile)
    index = (lambda n, m: (base + n, 0)) if turned else (lambda n, m: (0, base + n))
    return call(
        kernel,
        (half // tile,),
        [mask],
        [whole_spec(x.shape), pl.BlockSpec(shape, index)],
        [pl.BlockSpec((rows, tile), lambda n, m: (0, n))] * groups,
        [jax.ShapeDtypeStruct((rows, half), bf16)] * groups,
        [pltpu.VMEM(shape, bf16)],
        2 * groups * rows * depth * half,
        2 * (groups * rows * depth + depth * half + groups * rows * half),
        [x, weight],
        limit=24000,
    )


def back_project(parts, weight, mask, place, r, turned, base=None, last=True):
    groups = len(parts) // COLORS
    rows, half = parts[0].shape
    fan = half * COLORS
    depth = weight.shape[0] if turned else weight.shape[1]
    cols = depth // r
    tile = min(cols, 256)
    sub = cols // tile
    count = len(parts)
    extra = list(base) if base is not None else []
    kind = bf16 if last else f32

    def tile_at(s, u, place_ref):
        return (s ^ place_ref[0]) * sub + u

    def kernel(place_ref, mask_ref, *rest):
        part_refs, rest = rest[:count], rest[count:]
        w_ref, rest = rest[0], rest[1:]
        base_refs, rest = rest[: len(extra)], rest[len(extra) :]
        outs, (held, kept, sems) = rest[:r], rest[r:]
        s, u = pl.program_id(0), pl.program_id(1)

        @pl.when((s == 0) & (u == 0))
        def _():
            load_groups(part_refs, held, sems, rows, half)

        first = tile_at(s, u, place_ref) * (tile // BLK)
        if turned:
            keep_blocks(kept, lambda at: w_ref[at], mask_ref, first, 0)
        else:
            keep_blocks(kept, lambda at: w_ref[at], mask_ref, 0, first)
        total = dot(held[...], kept[...], NT if turned else NN).reshape(groups, rows, tile)
        for t in range(r):

            @pl.when(s == t)
            def _():
                value = total + base_refs[t][...] if extra else total
                outs[t][...] = value.astype(kind)

    def share(t):
        return lambda s, u, *_: (0, 0, jnp.where(s == t, u, jnp.where(s < t, 0, sub - 1)))

    shape = (tile, fan) if turned else (fan, tile)
    if turned:
        index = lambda s, u, pr, *_: (tile_at(s, u, pr), 0)
    else:
        index = lambda s, u, pr, *_: (0, tile_at(s, u, pr))
    shares = [pl.BlockSpec((groups, rows, tile), share(t)) for t in range(r)]
    return call(
        kernel,
        (r, sub),
        [place, mask],
        [ANY] * count + [pl.BlockSpec(shape, index)] + (shares if extra else []),
        shares,
        [jax.ShapeDtypeStruct((groups, rows, cols), kind)] * r,
        [
            pltpu.VMEM((groups * rows, fan), bf16),
            pltpu.VMEM(shape, bf16),
            pltpu.SemaphoreType.DMA((count,)),
        ],
        2 * groups * rows * depth * fan,
        2 * (groups * rows * fan + depth * fan) + 4 * groups * rows * depth,
        list(parts) + [weight] + extra,
    )


def outer_up(x, parts, mask, scale):
    groups, r, rows, cols = x.shape
    half = parts[0].shape[1]
    fan, depth = half * COLORS, r * cols
    tile = min(cols, 256)
    sub = cols // tile

    def kernel(mask_ref, x_ref, *rest):
        part_refs, (out, held, sems) = rest[: len(parts)], rest[len(parts) :]
        n = pl.program_id(0)

        @pl.when(n == 0)
        def _():
            load_groups(part_refs, held, sems, rows, half)

        left = x_ref[:, 0].reshape(groups * rows, tile)
        value = dot(left, held[...], TN) * scale
        keep_blocks(out, lambda at: value[at].astype(bf16), mask_ref, n * (tile // BLK), 0)

    return call(
        kernel,
        (depth // tile,),
        [mask],
        [pl.BlockSpec((groups, 1, rows, tile), lambda n, m: (0, n // sub, 0, n % sub))]
        + [ANY] * len(parts),
        pl.BlockSpec((tile, fan), lambda n, m: (n, 0)),
        jax.ShapeDtypeStruct((depth, fan), bf16),
        [pltpu.VMEM((groups * rows, fan), bf16), pltpu.SemaphoreType.DMA((len(parts),))],
        2 * groups * rows * depth * fan,
        2 * (groups * rows * (depth + fan) + depth * fan),
        [x] + list(parts),
    )


def outer_down(parts, x, mask, scale):
    groups, r, rows, cols = x.shape
    half = parts[0].shape[1]
    fan, depth = half * COLORS, r * cols
    tile = min(fan, 256)

    def kernel(mask_ref, x_ref, *rest):
        part_refs, (out, held, sems) = rest[: len(parts)], rest[len(parts) :]
        n = pl.program_id(0)

        @pl.when(n == 0)
        def _():
            load_groups(part_refs, held, sems, rows, half)

        left = held[:, pl.ds(pl.multiple_of(n * tile, tile), tile)]
        for c in range(r):
            value = dot(left, x_ref[:, c].reshape(groups * rows, cols), TN) * scale
            keep_blocks(
                out.at[:, pl.ds(c * cols, cols)],
                lambda at: value[at].astype(bf16),
                mask_ref,
                n * (tile // BLK),
                c * (cols // BLK),
            )

    return call(
        kernel,
        (fan // tile,),
        [mask],
        [whole_spec(x.shape)] + [ANY] * len(parts),
        pl.BlockSpec((tile, depth), lambda n, m: (n, 0)),
        jax.ShapeDtypeStruct((fan, depth), bf16),
        [pltpu.VMEM((groups * rows, fan), bf16), pltpu.SemaphoreType.DMA((len(parts),))],
        2 * groups * rows * depth * fan,
        2 * (groups * rows * (depth + fan) + depth * fan),
        [x] + list(parts),
    )


def assemble(pieces, where, groups, r):
    rows, cols = pieces[0][0].shape
    flat = [p for line in pieces for p in line]

    def kernel(where_ref, *rest):
        refs, (out, sems) = rest[: len(flat)], rest[len(flat) :]
        copies = []
        for n, ref in enumerate(refs):
            s, t = divmod(n, groups)
            dst = out.at[where_ref[0] ^ t, where_ref[1] ^ s]
            copies.append(pltpu.make_async_copy(ref, dst, sems.at[n]))
        for copy in copies:
            copy.start()
        for copy in copies:
            copy.wait()

    return call(
        kernel,
        (1,),
        [where],
        [ANY] * len(flat),
        whole_spec((groups, r, rows, cols)),
        jax.ShapeDtypeStruct((groups, r, rows, cols), bf16),
        [pltpu.SemaphoreType.DMA((len(flat),))],
        0,
        4 * len(flat) * rows * cols,
        flat,
    )


def body(tokens, cotangent, gate_weight, up_weight, down_weight, gate_mask, up_mask, down_mask):
    dp = lax.axis_size("dp")
    mp = lax.axis_size("mp")
    ratio = mp // dp
    bits = dp.bit_length() - 1
    rows = tokens.shape[0]
    scale = 1.0 / math.sqrt(rows * dp)
    there = []
    for i in range(dp):
        for j in range(mp):
            d, c = j // ratio, j % ratio
            there.append((i * mp + j, d * mp + ratio * (i ^ d) + c))
    back = [(b, a) for a, b in there]
    me = lax.axis_index("mp")
    my_k, my_c = me // ratio, me % ratio
    where = jnp.stack([my_k, my_c]).astype(jnp.int32)
    place = my_c.reshape(1).astype(jnp.int32)

    def over_mp(value, step):
        return lax.ppermute(value, "mp", [(j, j ^ step) for j in range(mp)])

    queues = [[] for _ in range(bits)]

    def over_dp(value, bit, *earlier):
        queue = queues[bit]
        earlier = list(earlier)
        if len(queue) >= DEPTH:
            earlier.append(queue[-DEPTH])
        if earlier:
            value = after(value, *earlier)
        queue.append(lax.ppermute(value, "dp", [(i, i ^ (1 << bit)) for i in range(dp)]))
        return queue[-1]

    def spread_rows(moved):
        line = [moved] + [over_mp(moved, ratio * t) for t in range(1, dp)]
        pieces = [line] + [[over_mp(v, s) for v in line] for s in range(1, ratio)]
        return assemble(pieces, where, dp, ratio), line

    def collect_rows(part):
        total = part[0].astype(f32)
        for s in range(1, ratio):
            total = total + over_mp(part[s], s).astype(f32)
        total = total.astype(bf16)
        own = lax.dynamic_index_in_dim(total, my_k, 0, keepdims=False).astype(f32)
        for t in range(1, dp):
            sent = lax.dynamic_index_in_dim(total, my_k ^ t, 0, keepdims=False)
            own = own + over_mp(sent, ratio * t).astype(f32)
        return lax.ppermute(own.astype(bf16), ("dp", "mp"), back)

    def order(color):
        return list(range(bits)) if color % 2 == 0 else list(range(bits))[::-1]

    def reduce_dp(parts):
        vals = [dict(enumerate(p)) for p in parts]
        for step in range(bits):
            for h, held in enumerate(vals):
                bit = order(h)[step]
                for k in sorted((k for k in held if k >> bit & 1), reverse=True):
                    got = over_dp(held.pop(k).astype(bf16), bit)
                    held[k ^ (1 << bit)] = held[k ^ (1 << bit)].astype(f32) + got.astype(f32)
        return [held[0] for held in vals]

    def gather_dp(own, holds=((), ())):
        vals = [{0: v} for v in own]
        for step in range(bits):
            hold = holds[min(step, 1)]
            for h, held in enumerate(vals):
                bit = order(h)[::-1][step]
                for k in sorted(held, reverse=True):
                    held[k ^ (1 << bit)] = over_dp(held[k], bit, *(hold if k else holds[0]))
        return [held[k] for held in vals for k in range(dp)]

    colors = range(COLORS)
    tok_moved = lax.ppermute(tokens, ("dp", "mp"), there)
    cot_moved = lax.ppermute(cotangent, ("dp", "mp"), there)
    tok, tok_line = spread_rows(tok_moved)
    gate_parts = [project(tok, gate_weight, gate_mask, h, False) for h in colors]
    tok_up = after(tok, *[p[0] for p in gate_parts])
    up_parts = [project(tok_up, up_weight, up_mask, h, False) for h in colors]
    cot, _ = spread_rows(after(cot_moved, *tok_line))
    grad_parts = [project(cot, down_weight, down_mask, h, True) for h in colors]
    gate_pre = reduce_dp(gate_parts)
    up_pre = reduce_dp(up_parts)
    hidden_grad = reduce_dp(grad_parts)
    own_hidden, own_gate, own_up = [], [], []
    for gate, up, grad in zip(gate_pre, up_pre, hidden_grad):
        sigmoid_gate = 1.0 / (1.0 + jnp.exp(-gate))
        activated = gate * sigmoid_gate
        own_hidden.append((activated * up).astype(bf16))
        slope = sigmoid_gate * (1.0 + gate * (1.0 - sigmoid_gate))
        own_gate.append((grad * up * slope).astype(bf16))
        own_up.append((grad * activated).astype(bf16))
    hidden = gather_dp(own_hidden)
    gate_delta = gather_dp(own_gate)
    out_part = back_project(hidden, down_weight, down_mask, place, ratio, False)
    down_grad = outer_down(hidden, cot, down_mask, scale)
    from_gate = back_project(
        gate_delta, gate_weight, gate_mask, place, ratio, True, last=False
    )
    up_delta = gather_dp(own_up, ((out_part[0],), (out_part[0], down_grad)))
    layer_out = collect_rows(out_part)
    late = after(up_delta[0], from_gate[0], layer_out)
    grad_part = back_project(
        [late] + up_delta[1:], up_weight, up_mask, place, ratio, True, base=from_gate
    )
    token_grad = collect_rows(grad_part)
    last_tok = after(tok, grad_part[0])
    gate_grad = outer_up(last_tok, gate_delta, gate_mask, scale)
    up_grad = outer_up(last_tok, up_delta, up_mask, scale)
    return (layer_out, token_grad, gate_grad, up_grad, down_grad)


def solution(mesh):
    placed = (
        P("dp", "mp"),
        P("dp", "mp"),
        P("dp", "mp"),
        P("dp", "mp"),
        P("mp", "dp"),
        P("dp", "mp"),
        P("dp", "mp"),
        P("mp", "dp"),
    )
    return jax.shard_map(
        body,
        mesh=mesh,
        in_specs=placed,
        out_specs=(P("dp", "mp"), P("dp", "mp"), P("dp", "mp"), P("dp", "mp"), P("mp", "dp")),
        check_vma=False,
    )
```

```python
import math

import jax
import jax.numpy as jnp
from jax import lax
from jax.experimental import pallas as pl
from jax.experimental.pallas import tpu as pltpu
from jax.sharding import PartitionSpec as P


BLK = 128
COLORS = 2
bf16, f32 = jnp.bfloat16, jnp.float32
NN = (((1,), (0,)), ((), ()))
NT = (((1,), (1,)), ((), ()))
TN = (((0,), (0,)), ((), ()))


DEPTH = 2
CHUNKS = 2


def after(value, *earlier):
    return lax.optimization_barrier((value,) + earlier)[0]


def dot(a, b, dims):
    return lax.dot_general(a, b, dims, preferred_element_type=f32)


def keep_blocks(dst, value_of, mask, row0, col0):
    for rb in range(dst.shape[0] // BLK):
        for cb in range(dst.shape[1] // BLK):
            at = (slice(rb * BLK, (rb + 1) * BLK), slice(cb * BLK, (cb + 1) * BLK))
            block = value_of(at)
            dst[at] = jnp.where(mask[row0 + rb, col0 + cb] != 0, block, jnp.zeros_like(block))


def load_groups(places, sems):
    copies = [pltpu.make_async_copy(src, dst, sems.at[n]) for n, (src, dst) in enumerate(places)]
    for copy in copies:
        copy.start()
    for copy in copies:
        copy.wait()


def by_group(refs, held, rows, half):
    groups = len(refs) // COLORS
    places = []
    for n, ref in enumerate(refs):
        color, k = divmod(n, groups)
        places.append((ref, held.at[pl.ds(k * rows, rows), pl.ds(color * half, half)]))
    return places


def by_chunk(refs, pick, held, rows, half, chunks):
    per = len(refs) // chunks
    groups = per // COLORS
    places = []
    for n, ref in enumerate(refs):
        j, rest = divmod(n, per)
        color, k = divmod(rest, groups)
        at = pl.ds((k * chunks + j) * rows, rows)
        places.append((ref.at[pick], held.at[at, pl.ds(color * half, half)]))
    return places


def call(kernel, grid, prefetch, in_specs, out_specs, out_shape, scratch, flops, nbytes, args, limit=40000):
    return pl.pallas_call(
        kernel,
        grid_spec=pltpu.PrefetchScalarGridSpec(
            num_scalar_prefetch=len(prefetch),
            grid=grid,
            in_specs=in_specs,
            out_specs=out_specs,
            scratch_shapes=scratch,
        ),
        out_shape=out_shape,
        compiler_params=pltpu.CompilerParams(
            dimension_semantics=("arbitrary",) * len(grid), vmem_limit_bytes=limit << 10
        ),
        cost_estimate=pl.CostEstimate(flops=flops, transcendentals=0, bytes_accessed=nbytes),
    )(*prefetch, *args)


def whole_spec(shape):
    return pl.BlockSpec(shape, lambda *_: (0,) * len(shape))


ANY = pl.BlockSpec(memory_space=pl.ANY)


def project(x, weight, mask, color, turned):
    groups, r, rows, cols = x.shape
    depth, fan = weight.shape[::-1] if turned else weight.shape
    half = fan // COLORS
    tile = min(half, 512)
    base = color * half // tile

    def kernel(mask_ref, x_ref, w_ref, *rest):
        outs, kept = rest[:groups], rest[groups]
        first = (base + pl.program_id(0)) * (tile // BLK)
        if turned:
            keep_blocks(kept, lambda at: w_ref[at], mask_ref, first, 0)
        else:
            keep_blocks(kept, lambda at: w_ref[at], mask_ref, 0, first)
        total = None
        for c in range(r):
            left = x_ref[:, c].reshape(groups * rows, cols)
            span = slice(c * cols, (c + 1) * cols)
            term = dot(left, kept[:, span], NT) if turned else dot(left, kept[span, :], NN)
            total = term if total is None else total + term
        for k in range(groups):
            outs[k][...] = total[k * rows : (k + 1) * rows].astype(bf16)

    shape = (tile, depth) if turned else (depth, tile)
    index = (lambda n, m: (base + n, 0)) if turned else (lambda n, m: (0, base + n))
    return call(
        kernel,
        (half // tile,),
        [mask],
        [whole_spec(x.shape), pl.BlockSpec(shape, index)],
        [pl.BlockSpec((rows, tile), lambda n, m: (0, n))] * groups,
        [jax.ShapeDtypeStruct((rows, half), bf16)] * groups,
        [pltpu.VMEM(shape, bf16)],
        2 * groups * rows * depth * half,
        2 * (groups * rows * depth + depth * half + groups * rows * half),
        [x, weight],
        limit=24000,
    )


def back_project(parts, weights, masks, place, r, turned):
    groups = len(parts) // COLORS
    rows, half = parts[0].shape[-2:]
    fan = half * COLORS
    depth = weights[0].shape[0] if turned else weights[0].shape[1]
    cols = depth // r
    tile = min(cols, 256)
    sub = cols // tile
    count, several = len(parts), len(weights)

    def tile_at(s, u, place_ref):
        return (s ^ place_ref[0]) * sub + u

    def kernel(place_ref, *rest):
        mask_refs, rest = rest[:several], rest[several:]
        part_refs, rest = rest[:count], rest[count:]
        w_refs, rest = rest[:several], rest[several:]
        outs, rest = rest[:r], rest[r:]
        helds, kepts, sems = rest[:several], rest[several : 2 * several], rest[2 * several]
        s, u = pl.program_id(0), pl.program_id(1)

        @pl.when((s == 0) & (u == 0))
        def _():
            places = []
            for i in range(several):
                if several > 1:
                    places += by_chunk(part_refs, i, helds[i], rows, half, 1)
                else:
                    places += by_group(part_refs, helds[i], rows, half)
            load_groups(places, sems)

        first = tile_at(s, u, place_ref) * (tile // BLK)
        total = None
        for i in range(several):
            w_ref = w_refs[i]
            where = (first, 0) if turned else (0, first)
            keep_blocks(kepts[i], lambda at: w_ref[at], mask_refs[i], *where)
            term = dot(helds[i][...], kepts[i][...], NT if turned else NN)
            total = term if total is None else total + term
        total = total.astype(bf16).reshape(groups, rows, tile)
        for t in range(r):

            @pl.when(s == t)
            def _():
                outs[t][...] = total

    def share(t):
        return lambda s, u, *_: (0, 0, jnp.where(s == t, u, jnp.where(s < t, 0, sub - 1)))

    shape = (tile, fan) if turned else (fan, tile)
    if turned:
        index = lambda s, u, pr, *_: (tile_at(s, u, pr), 0)
    else:
        index = lambda s, u, pr, *_: (0, tile_at(s, u, pr))
    return call(
        kernel,
        (r, sub),
        [place] + masks,
        [ANY] * count + [pl.BlockSpec(shape, index)] * several,
        [pl.BlockSpec((groups, rows, tile), share(t)) for t in range(r)],
        [jax.ShapeDtypeStruct((groups, rows, cols), bf16)] * r,
        [pltpu.VMEM((groups * rows, fan), bf16)] * several
        + [pltpu.VMEM(shape, bf16)] * several
        + [pltpu.SemaphoreType.DMA((count * several,))],
        2 * several * groups * rows * depth * fan,
        2 * several * (groups * rows * fan + depth * fan) + 2 * groups * rows * depth,
        list(parts) + list(weights),
    )


def outer_up(x, parts, pick, chunks, mask, scale):
    groups, r, rows, cols = x.shape
    half = parts[0].shape[-1]
    fan, depth = half * COLORS, r * cols
    tile = min(cols, 256)
    sub = cols // tile

    def kernel(mask_ref, x_ref, *rest):
        part_refs, (out, held, sems) = rest[: len(parts)], rest[len(parts) :]
        n = pl.program_id(0)

        @pl.when(n == 0)
        def _():
            load_groups(by_chunk(part_refs, pick, held, rows // chunks, half, chunks), sems)

        left = x_ref[:, 0].reshape(groups * rows, tile)
        value = dot(left, held[...], TN) * scale
        keep_blocks(out, lambda at: value[at].astype(bf16), mask_ref, n * (tile // BLK), 0)

    return call(
        kernel,
        (depth // tile,),
        [mask],
        [pl.BlockSpec((groups, 1, rows, tile), lambda n, m: (0, n // sub, 0, n % sub))]
        + [ANY] * len(parts),
        pl.BlockSpec((tile, fan), lambda n, m: (n, 0)),
        jax.ShapeDtypeStruct((depth, fan), bf16),
        [pltpu.VMEM((groups * rows, fan), bf16), pltpu.SemaphoreType.DMA((len(parts),))],
        2 * groups * rows * depth * fan,
        2 * (groups * rows * (depth + fan) + depth * fan),
        [x] + list(parts),
    )


def outer_down(parts, x, mask, scale):
    groups, r, rows, cols = x.shape
    half = parts[0].shape[1]
    fan, depth = half * COLORS, r * cols
    tile = min(fan, 256)

    def kernel(mask_ref, x_ref, *rest):
        part_refs, (out, held, sems) = rest[: len(parts)], rest[len(parts) :]
        n = pl.program_id(0)

        @pl.when(n == 0)
        def _():
            load_groups(by_group(part_refs, held, rows, half), sems)

        left = held[:, pl.ds(pl.multiple_of(n * tile, tile), tile)]
        for c in range(r):
            value = dot(left, x_ref[:, c].reshape(groups * rows, cols), TN) * scale
            keep_blocks(
                out.at[:, pl.ds(c * cols, cols)],
                lambda at: value[at].astype(bf16),
                mask_ref,
                n * (tile // BLK),
                c * (cols // BLK),
            )

    return call(
        kernel,
        (fan // tile,),
        [mask],
        [whole_spec(x.shape)] + [ANY] * len(parts),
        pl.BlockSpec((tile, depth), lambda n, m: (n, 0)),
        jax.ShapeDtypeStruct((fan, depth), bf16),
        [pltpu.VMEM((groups * rows, fan), bf16), pltpu.SemaphoreType.DMA((len(parts),))],
        2 * groups * rows * depth * fan,
        2 * (groups * rows * (depth + fan) + depth * fan),
        [x] + list(parts),
    )


def assemble(pieces, where, groups, r):
    rows, cols = pieces[0][0].shape
    flat = [p for line in pieces for p in line]

    def kernel(where_ref, *rest):
        refs, (out, sems) = rest[: len(flat)], rest[len(flat) :]
        copies = []
        for n, ref in enumerate(refs):
            s, t = divmod(n, groups)
            dst = out.at[where_ref[0] ^ t, where_ref[1] ^ s]
            copies.append(pltpu.make_async_copy(ref, dst, sems.at[n]))
        for copy in copies:
            copy.start()
        for copy in copies:
            copy.wait()

    return call(
        kernel,
        (1,),
        [where],
        [ANY] * len(flat),
        whole_spec((groups, r, rows, cols)),
        jax.ShapeDtypeStruct((groups, r, rows, cols), bf16),
        [pltpu.SemaphoreType.DMA((len(flat),))],
        0,
        4 * len(flat) * rows * cols,
        flat,
    )


def body(tokens, cotangent, gate_weight, up_weight, down_weight, gate_mask, up_mask, down_mask):
    dp = lax.axis_size("dp")
    mp = lax.axis_size("mp")
    ratio = mp // dp
    bits = dp.bit_length() - 1
    rows = tokens.shape[0]
    scale = 1.0 / math.sqrt(rows * dp)
    there = []
    for i in range(dp):
        for j in range(mp):
            d, c = j // ratio, j % ratio
            there.append((i * mp + j, d * mp + ratio * (i ^ d) + c))
    back = [(b, a) for a, b in there]
    me = lax.axis_index("mp")
    my_k, my_c = me // ratio, me % ratio
    where = jnp.stack([my_k, my_c]).astype(jnp.int32)
    place = my_c.reshape(1).astype(jnp.int32)

    def over_mp(value, step):
        return lax.ppermute(value, "mp", [(j, j ^ step) for j in range(mp)])

    queues = [[] for _ in range(bits)]

    def over_dp(value, bit, *earlier):
        queue = queues[bit]
        earlier = list(earlier)
        if len(queue) >= DEPTH:
            earlier.append(queue[-DEPTH])
        if earlier:
            value = after(value, *earlier)
        queue.append(lax.ppermute(value, "dp", [(i, i ^ (1 << bit)) for i in range(dp)]))
        return queue[-1]

    def spread_rows(moved):
        line = [moved] + [over_mp(moved, ratio * t) for t in range(1, dp)]
        pieces = [line] + [[over_mp(v, s) for v in line] for s in range(1, ratio)]
        return assemble(pieces, where, dp, ratio), line

    def collect_rows(part):
        total = part[0].astype(f32)
        for s in range(1, ratio):
            total = total + over_mp(part[s], s).astype(f32)
        total = total.astype(bf16)
        own = lax.dynamic_index_in_dim(total, my_k, 0, keepdims=False).astype(f32)
        for t in range(1, dp):
            sent = lax.dynamic_index_in_dim(total, my_k ^ t, 0, keepdims=False)
            own = own + over_mp(sent, ratio * t).astype(f32)
        return lax.ppermute(own.astype(bf16), ("dp", "mp"), back)

    def order(color):
        return list(range(bits)) if color % 2 == 0 else list(range(bits))[::-1]

    def reduce_dp(parts):
        vals = [dict(enumerate(p)) for p in parts]
        for step in range(bits):
            for h, held in enumerate(vals):
                bit = order(h)[step]
                for k in sorted((k for k in held if k >> bit & 1), reverse=True):
                    got = over_dp(held.pop(k).astype(bf16), bit)
                    held[k ^ (1 << bit)] = held[k ^ (1 << bit)].astype(f32) + got.astype(f32)
        return [held[0] for held in vals]

    def gather_dp(own, first=(), second=(), relay=()):
        vals = [{0: v} for v in own]
        for step in range(bits):
            for h, held in enumerate(vals):
                bit = order(h)[::-1][step]
                for k in sorted(held):
                    hold = first if step == 0 else relay if k else second
                    slot = k ^ (1 << bit)
                    held[slot] = over_dp(held[k], bit, *hold)
        return [held[k] for held in vals for k in range(dp)]

    colors = range(COLORS)
    tok_moved = lax.ppermute(tokens, ("dp", "mp"), there)
    cot_moved = lax.ppermute(cotangent, ("dp", "mp"), there)
    tok, tok_line = spread_rows(tok_moved)
    gate_parts = [project(tok, gate_weight, gate_mask, h, False) for h in colors]
    tok_up = after(tok, *[p[0] for p in gate_parts])
    up_parts = [project(tok_up, up_weight, up_mask, h, False) for h in colors]
    cot, _ = spread_rows(after(cot_moved, *tok_line, up_parts[0][0]))
    grad_parts = [project(cot, down_weight, down_mask, h, True) for h in colors]
    gate_pre = reduce_dp(gate_parts)
    up_pre = reduce_dp(up_parts)
    hidden_grad = reduce_dp(grad_parts)
    own_hidden, own_delta = [], [[] for _ in range(CHUNKS)]
    step = rows // CHUNKS
    for gate, up, grad in zip(gate_pre, up_pre, hidden_grad):
        sigmoid_gate = 1.0 / (1.0 + jnp.exp(-gate))
        activated = gate * sigmoid_gate
        own_hidden.append((activated * up).astype(bf16))
        slope = sigmoid_gate * (1.0 + gate * (1.0 - sigmoid_gate))
        gate_delta = (grad * up * slope).astype(bf16)
        up_delta = (grad * activated).astype(bf16)
        for j in range(CHUNKS):
            at = slice(j * step, (j + 1) * step)
            own_delta[j].append(jnp.stack([gate_delta[at], up_delta[at]]))
    hidden = gather_dp(own_hidden)
    out_part = back_project(hidden, [down_weight], [down_mask], place, ratio, False)
    down_grad = outer_down(hidden, cot, down_mask, scale)
    layer_out = collect_rows(out_part)
    deltas, token_grad, done = [], [], ()
    for j in range(CHUNKS):
        if j == 0:
            delta = gather_dp(own_delta[j])
        else:
            delta = gather_dp(own_delta[j], (), (out_part[0],), (out_part[0], down_grad))
        first = after(delta[0], *done)
        part = back_project(
            [first] + delta[1:],
            [gate_weight, up_weight],
            [gate_mask, up_mask],
            place,
            ratio,
            True,
        )
        token_grad.append(collect_rows(part))
        deltas += delta
        done = (layer_out, part[0])
    last_tok = after(tok, part[0])
    gate_grad = outer_up(last_tok, deltas, 0, CHUNKS, gate_mask, scale)
    up_grad = outer_up(last_tok, deltas, 1, CHUNKS, up_mask, scale)
    token_grad = jnp.concatenate(token_grad, axis=0)
    return (layer_out, token_grad, gate_grad, up_grad, down_grad)


def solution(mesh):
    placed = (
        P("dp", "mp"),
        P("dp", "mp"),
        P("dp", "mp"),
        P("dp", "mp"),
        P("mp", "dp"),
        P("dp", "mp"),
        P("dp", "mp"),
        P("mp", "dp"),
    )

    return jax.shard_map(
        body,
        mesh=mesh,
        in_specs=placed,
        out_specs=(P("dp", "mp"), P("dp", "mp"), P("dp", "mp"), P("dp", "mp"), P("mp", "dp")),
        check_vma=False,
    )
```

```python
import math

import jax
import jax.numpy as jnp
from jax import lax
from jax.experimental import pallas as pl
from jax.experimental.pallas import tpu as pltpu
from jax.sharding import PartitionSpec as P


BLK = 128
COLORS = 2
bf16, f32 = jnp.bfloat16, jnp.float32
NN = (((1,), (0,)), ((), ()))
NT = (((1,), (1,)), ((), ()))
TN = (((0,), (0,)), ((), ()))


DEPTH = 2
CHUNKS = 2


def after(value, *earlier):
    return lax.optimization_barrier((value,) + earlier)[0]


def dot(a, b, dims):
    return lax.dot_general(a, b, dims, preferred_element_type=f32)


def keep_blocks(dst, value_of, mask, row0, col0):
    for rb in range(dst.shape[0] // BLK):
        for cb in range(dst.shape[1] // BLK):
            at = (slice(rb * BLK, (rb + 1) * BLK), slice(cb * BLK, (cb + 1) * BLK))
            block = value_of(at)
            dst[at] = jnp.where(mask[row0 + rb, col0 + cb] != 0, block, jnp.zeros_like(block))


def load_groups(places, sems):
    copies = [pltpu.make_async_copy(src, dst, sems.at[n]) for n, (src, dst) in enumerate(places)]
    for copy in copies:
        copy.start()
    for copy in copies:
        copy.wait()


def by_group(refs, held, rows, half):
    groups = len(refs) // COLORS
    places = []
    for n, ref in enumerate(refs):
        color, k = divmod(n, groups)
        places.append((ref, held.at[pl.ds(k * rows, rows), pl.ds(color * half, half)]))
    return places


def by_chunk(refs, pick, held, rows, half, chunks):
    per = len(refs) // chunks
    groups = per // COLORS
    places = []
    for n, ref in enumerate(refs):
        j, rest = divmod(n, per)
        color, k = divmod(rest, groups)
        at = pl.ds((k * chunks + j) * rows, rows)
        places.append((ref.at[pick], held.at[at, pl.ds(color * half, half)]))
    return places


def call(kernel, grid, prefetch, in_specs, out_specs, out_shape, scratch, flops, nbytes, args, limit=40000):
    return pl.pallas_call(
        kernel,
        grid_spec=pltpu.PrefetchScalarGridSpec(
            num_scalar_prefetch=len(prefetch),
            grid=grid,
            in_specs=in_specs,
            out_specs=out_specs,
            scratch_shapes=scratch,
        ),
        out_shape=out_shape,
        compiler_params=pltpu.CompilerParams(
            dimension_semantics=("arbitrary",) * len(grid), vmem_limit_bytes=limit << 10
        ),
        cost_estimate=pl.CostEstimate(flops=flops, transcendentals=0, bytes_accessed=nbytes),
    )(*prefetch, *args)


def whole_spec(shape):
    return pl.BlockSpec(shape, lambda *_: (0,) * len(shape))


ANY = pl.BlockSpec(memory_space=pl.ANY)


def project(x, weight, mask, color, turned):
    groups, r, rows, cols = x.shape
    depth, fan = weight.shape[::-1] if turned else weight.shape
    half = fan // COLORS
    tile = min(half, 512)
    base = color * half // tile

    def kernel(mask_ref, x_ref, w_ref, *rest):
        outs, kept = rest[:groups], rest[groups]
        first = (base + pl.program_id(0)) * (tile // BLK)
        if turned:
            keep_blocks(kept, lambda at: w_ref[at], mask_ref, first, 0)
        else:
            keep_blocks(kept, lambda at: w_ref[at], mask_ref, 0, first)
        total = None
        for c in range(r):
            left = x_ref[:, c].reshape(groups * rows, cols)
            span = slice(c * cols, (c + 1) * cols)
            term = dot(left, kept[:, span], NT) if turned else dot(left, kept[span, :], NN)
            total = term if total is None else total + term
        for k in range(groups):
            outs[k][...] = total[k * rows : (k + 1) * rows].astype(bf16)

    shape = (tile, depth) if turned else (depth, tile)
    index = (lambda n, m: (base + n, 0)) if turned else (lambda n, m: (0, base + n))
    return call(
        kernel,
        (half // tile,),
        [mask],
        [whole_spec(x.shape), pl.BlockSpec(shape, index)],
        [pl.BlockSpec((rows, tile), lambda n, m: (0, n))] * groups,
        [jax.ShapeDtypeStruct((rows, half), bf16)] * groups,
        [pltpu.VMEM(shape, bf16)],
        2 * groups * rows * depth * half,
        2 * (groups * rows * depth + depth * half + groups * rows * half),
        [x, weight],
        limit=24000,
    )


def back_project(parts, weights, masks, place, r, turned):
    groups = len(parts) // COLORS
    rows, half = parts[0].shape[-2:]
    fan = half * COLORS
    depth = weights[0].shape[0] if turned else weights[0].shape[1]
    cols = depth // r
    tile = min(cols, 256)
    sub = cols // tile
    count, several = len(parts), len(weights)

    def tile_at(s, u, place_ref):
        return (s ^ place_ref[0]) * sub + u

    def kernel(place_ref, *rest):
        mask_refs, rest = rest[:several], rest[several:]
        part_refs, rest = rest[:count], rest[count:]
        w_refs, rest = rest[:several], rest[several:]
        outs, rest = rest[:r], rest[r:]
        helds, kepts, sems = rest[:several], rest[several : 2 * several], rest[2 * several]
        s, u = pl.program_id(0), pl.program_id(1)

        @pl.when((s == 0) & (u == 0))
        def _():
            places = []
            for i in range(several):
                if several > 1:
                    places += by_chunk(part_refs, i, helds[i], rows, half, 1)
                else:
                    places += by_group(part_refs, helds[i], rows, half)
            load_groups(places, sems)

        first = tile_at(s, u, place_ref) * (tile // BLK)
        total = None
        for i in range(several):
            w_ref = w_refs[i]
            where = (first, 0) if turned else (0, first)
            keep_blocks(kepts[i], lambda at: w_ref[at], mask_refs[i], *where)
            term = dot(helds[i][...], kepts[i][...], NT if turned else NN)
            total = term if total is None else total + term
        total = total.astype(bf16).reshape(groups, rows, tile)
        for t in range(r):

            @pl.when(s == t)
            def _():
                outs[t][...] = total

    def share(t):
        return lambda s, u, *_: (0, 0, jnp.where(s == t, u, jnp.where(s < t, 0, sub - 1)))

    shape = (tile, fan) if turned else (fan, tile)
    if turned:
        index = lambda s, u, pr, *_: (tile_at(s, u, pr), 0)
    else:
        index = lambda s, u, pr, *_: (0, tile_at(s, u, pr))
    return call(
        kernel,
        (r, sub),
        [place] + masks,
        [ANY] * count + [pl.BlockSpec(shape, index)] * several,
        [pl.BlockSpec((groups, rows, tile), share(t)) for t in range(r)],
        [jax.ShapeDtypeStruct((groups, rows, cols), bf16)] * r,
        [pltpu.VMEM((groups * rows, fan), bf16)] * several
        + [pltpu.VMEM(shape, bf16)] * several
        + [pltpu.SemaphoreType.DMA((count * several,))],
        2 * several * groups * rows * depth * fan,
        2 * several * (groups * rows * fan + depth * fan) + 2 * groups * rows * depth,
        list(parts) + list(weights),
    )


def outer_up(x, parts, pick, chunks, mask, scale):
    groups, r, rows, cols = x.shape
    half = parts[0].shape[-1]
    fan, depth = half * COLORS, r * cols
    tile = min(cols, 256)
    sub = cols // tile

    def kernel(mask_ref, x_ref, *rest):
        part_refs, (out, held, sems) = rest[: len(parts)], rest[len(parts) :]
        n = pl.program_id(0)

        @pl.when(n == 0)
        def _():
            load_groups(by_chunk(part_refs, pick, held, rows // chunks, half, chunks), sems)

        left = x_ref[:, 0].reshape(groups * rows, tile)
        value = dot(left, held[...], TN) * scale
        keep_blocks(out, lambda at: value[at].astype(bf16), mask_ref, n * (tile // BLK), 0)

    return call(
        kernel,
        (depth // tile,),
        [mask],
        [pl.BlockSpec((groups, 1, rows, tile), lambda n, m: (0, n // sub, 0, n % sub))]
        + [ANY] * len(parts),
        pl.BlockSpec((tile, fan), lambda n, m: (n, 0)),
        jax.ShapeDtypeStruct((depth, fan), bf16),
        [pltpu.VMEM((groups * rows, fan), bf16), pltpu.SemaphoreType.DMA((len(parts),))],
        2 * groups * rows * depth * fan,
        2 * (groups * rows * (depth + fan) + depth * fan),
        [x] + list(parts),
    )


def outer_down(parts, x, mask, scale):
    groups, r, rows, cols = x.shape
    half = parts[0].shape[1]
    fan, depth = half * COLORS, r * cols
    tile = min(fan, 256)

    def kernel(mask_ref, x_ref, *rest):
        part_refs, (out, held, sems) = rest[: len(parts)], rest[len(parts) :]
        n = pl.program_id(0)

        @pl.when(n == 0)
        def _():
            load_groups(by_group(part_refs, held, rows, half), sems)

        left = held[:, pl.ds(pl.multiple_of(n * tile, tile), tile)]
        for c in range(r):
            value = dot(left, x_ref[:, c].reshape(groups * rows, cols), TN) * scale
            keep_blocks(
                out.at[:, pl.ds(c * cols, cols)],
                lambda at: value[at].astype(bf16),
                mask_ref,
                n * (tile // BLK),
                c * (cols // BLK),
            )

    return call(
        kernel,
        (fan // tile,),
        [mask],
        [whole_spec(x.shape)] + [ANY] * len(parts),
        pl.BlockSpec((tile, depth), lambda n, m: (n, 0)),
        jax.ShapeDtypeStruct((fan, depth), bf16),
        [pltpu.VMEM((groups * rows, fan), bf16), pltpu.SemaphoreType.DMA((len(parts),))],
        2 * groups * rows * depth * fan,
        2 * (groups * rows * (depth + fan) + depth * fan),
        [x] + list(parts),
    )


def assemble(pieces, where, groups, r):
    rows, cols = pieces[0][0].shape
    flat = [p for line in pieces for p in line]

    def kernel(where_ref, *rest):
        refs, (out, sems) = rest[: len(flat)], rest[len(flat) :]
        copies = []
        for n, ref in enumerate(refs):
            s, t = divmod(n, groups)
            dst = out.at[where_ref[0] ^ t, where_ref[1] ^ s]
            copies.append(pltpu.make_async_copy(ref, dst, sems.at[n]))
        for copy in copies:
            copy.start()
        for copy in copies:
            copy.wait()

    return call(
        kernel,
        (1,),
        [where],
        [ANY] * len(flat),
        whole_spec((groups, r, rows, cols)),
        jax.ShapeDtypeStruct((groups, r, rows, cols), bf16),
        [pltpu.SemaphoreType.DMA((len(flat),))],
        0,
        4 * len(flat) * rows * cols,
        flat,
    )


def body(tokens, cotangent, gate_weight, up_weight, down_weight, gate_mask, up_mask, down_mask):
    dp = lax.axis_size("dp")
    mp = lax.axis_size("mp")
    ratio = mp // dp
    bits = dp.bit_length() - 1
    rows = tokens.shape[0]
    scale = 1.0 / math.sqrt(rows * dp)
    there = []
    for i in range(dp):
        for j in range(mp):
            d, c = j // ratio, j % ratio
            there.append((i * mp + j, d * mp + ratio * (i ^ d) + c))
    back = [(b, a) for a, b in there]
    me = lax.axis_index("mp")
    my_k, my_c = me // ratio, me % ratio
    where = jnp.stack([my_k, my_c]).astype(jnp.int32)
    place = my_c.reshape(1).astype(jnp.int32)

    def over_mp(value, step):
        return lax.ppermute(value, "mp", [(j, j ^ step) for j in range(mp)])

    queues = [[] for _ in range(bits)]

    def over_dp(value, bit, *earlier):
        queue = queues[bit]
        earlier = list(earlier)
        if len(queue) >= DEPTH:
            earlier.append(queue[-DEPTH])
        if earlier:
            value = after(value, *earlier)
        queue.append(lax.ppermute(value, "dp", [(i, i ^ (1 << bit)) for i in range(dp)]))
        return queue[-1]

    def spread_rows(moved):
        line = [moved] + [over_mp(moved, ratio * t) for t in range(1, dp)]
        pieces = [line] + [[over_mp(v, s) for v in line] for s in range(1, ratio)]
        return assemble(pieces, where, dp, ratio), line

    def collect_rows(part):
        total = part[0].astype(f32)
        for s in range(1, ratio):
            total = total + over_mp(part[s], s).astype(f32)
        total = total.astype(bf16)
        own = lax.dynamic_index_in_dim(total, my_k, 0, keepdims=False).astype(f32)
        for t in range(1, dp):
            sent = lax.dynamic_index_in_dim(total, my_k ^ t, 0, keepdims=False)
            own = own + over_mp(sent, ratio * t).astype(f32)
        return lax.ppermute(own.astype(bf16), ("dp", "mp"), back)

    def order(color):
        return list(range(bits)) if color % 2 == 0 else list(range(bits))[::-1]

    def reduce_dp(parts):
        vals = [dict(enumerate(p)) for p in parts]
        for step in range(bits):
            for h, held in enumerate(vals):
                bit = order(h)[step]
                for k in sorted((k for k in held if k >> bit & 1), reverse=True):
                    got = over_dp(held.pop(k).astype(bf16), bit)
                    held[k ^ (1 << bit)] = held[k ^ (1 << bit)].astype(f32) + got.astype(f32)
        return [held[0] for held in vals]

    def gather_dp(own, first=(), second=(), relay=()):
        vals = [{0: v} for v in own]
        for step in range(bits):
            for h, held in enumerate(vals):
                bit = order(h)[::-1][step]
                for k in sorted(held):
                    hold = first if step == 0 else relay if k else second
                    slot = k ^ (1 << bit)
                    held[slot] = over_dp(held[k], bit, *hold)
        return [held[k] for held in vals for k in range(dp)]

    colors = range(COLORS)
    tok_moved = lax.ppermute(tokens, ("dp", "mp"), there)
    cot_moved = lax.ppermute(cotangent, ("dp", "mp"), there)
    tok, tok_line = spread_rows(tok_moved)
    gate_parts = [project(tok, gate_weight, gate_mask, h, False) for h in colors]
    tok_up = after(tok, *[p[0] for p in gate_parts])
    up_parts = []
    for h in colors:
        up_parts.append(project(tok_up, up_weight, up_mask, h, False))
    cot, _ = spread_rows(after(cot_moved, *tok_line, up_parts[0][0]))
    grad_parts = [project(cot, down_weight, down_mask, h, True) for h in colors]
    gate_pre = reduce_dp(gate_parts)
    up_pre = reduce_dp(up_parts)
    hidden_grad = reduce_dp(grad_parts)
    own_hidden, own_delta = [], [[] for _ in range(CHUNKS)]
    step = rows // CHUNKS
    for gate, up, grad in zip(gate_pre, up_pre, hidden_grad):
        sigmoid_gate = 1.0 / (1.0 + jnp.exp(-gate))
        activated = gate * sigmoid_gate
        own_hidden.append((activated * up).astype(bf16))
        slope = sigmoid_gate * (1.0 + gate * (1.0 - sigmoid_gate))
        gate_delta = (grad * up * slope).astype(bf16)
        up_delta = (grad * activated).astype(bf16)
        for j in range(CHUNKS):
            at = slice(j * step, (j + 1) * step)
            own_delta[j].append(jnp.stack([gate_delta[at], up_delta[at]]))
    hidden = gather_dp(own_hidden)
    out_part = back_project(hidden, [down_weight], [down_mask], place, ratio, False)
    down_grad = outer_down(hidden, cot, down_mask, scale)
    layer_out = collect_rows(out_part)
    deltas, token_grad, done = [], [], ()
    for j in range(CHUNKS):
        if j == 0:
            delta = gather_dp(own_delta[j])
        else:
            delta = gather_dp(own_delta[j], (), (out_part[0],), (out_part[0], down_grad))
        first = after(delta[0], *done)
        part = back_project(
            [first] + delta[1:],
            [gate_weight, up_weight],
            [gate_mask, up_mask],
            place,
            ratio,
            True,
        )
        token_grad.append(collect_rows(part))
        deltas += delta
        done = (part[0],)
    last_tok = after(tok, part[0])
    gate_grad = outer_up(last_tok, deltas, 0, CHUNKS, gate_mask, scale)
    up_grad = outer_up(last_tok, deltas, 1, CHUNKS, up_mask, scale)
    token_grad = jnp.concatenate(token_grad, axis=0)
    return (layer_out, token_grad, gate_grad, up_grad, down_grad)


def solution(mesh):
    placed = (
        P("dp", "mp"),
        P("dp", "mp"),
        P("dp", "mp"),
        P("dp", "mp"),
        P("mp", "dp"),
        P("dp", "mp"),
        P("dp", "mp"),
        P("mp", "dp"),
    )

    return jax.shard_map(
        body,
        mesh=mesh,
        in_specs=placed,
        out_specs=(P("dp", "mp"), P("dp", "mp"), P("dp", "mp"), P("dp", "mp"), P("mp", "dp")),
        check_vma=False,
    )
```
